32 devices in a mesh: gx: 4 (over x, core), gy: 8 (over z, y).
Axes of the slice: x: 2, y: 2, z: 4, core: 2. Of those that a mesh axis runs over, the one named last changes fastest.
Arguments:
- points: bfloat16 [2048, 3, 256], P(('gx', 'gy')), may hold values from 0 to 1
- charges: bfloat16 [2048, 16, 256], P(('gx', 'gy')), may hold values from -6 to 6
- near_list: int32 [2048, 8], P(('gx', 'gy')), may hold values from 0 to 2047, as said below
- near_count: int32 [2048], P(('gx', 'gy')), may hold values from 1 to 8
- far_leaf: int32 [2048, 8], P(('gx', 'gy')), may hold values from 0 to 2047, as said below
- far_cluster: int32 [256, 8], P(('gx', 'gy')), may hold values from 0 to 255, as said below
- basis: bfloat16 [2048, 64, 256], P(('gx', 'gy')), may hold values from -0.375 to 0.375
- leaf_transfer: bfloat16 [2048, 4096], P(('gx', 'gy')), may hold values from -0.5 to 0.5
- cluster_transfer: bfloat16 [256, 4096], P(('gx', 'gy')), may hold values from -0.5 to 0.5
- leaf_coupling: bfloat16 [2048, 8, 4096], P(('gx', 'gy')), may hold values from -0.25 to 0.25
- cluster_coupling: bfloat16 [256, 8, 4096], P(('gx', 'gy')), may hold values from -0.25 to 0.25
- top_transfer: bfloat16 [2, 64, 64], replicated, may hold values from -0.5 to 0.5
- top_coupling: bfloat16 [2, 64, 64], replicated, may hold values from -0.75 to 0.75
Outputs:
- potential: float32 [2048, 16, 256], P(('gx', 'gy'))
The draws below stay inside these ranges and needn't reach their ends.
Inputs may be any that keep to these rules, and one draw needn't show every extreme that they name: `near_list`: every entry of row i is within 64 of i, and entry 0 is i itself. Slots of near_list from near_count on are not used. `far_leaf`: every entry of row i is within 64 of i. `far_cluster`: every entry of row c is within 8 of c.
All inputs are finite; a program needn't handle non-finite values.
Results may differ from the reference program's by a relative error of at most 0.0095.
Values may be sent and summed in bfloat16 or wider, within the bound.
A program may use at most 64 MiB of HBM per device.

```python
import jax
import jax.numpy as jnp
from jax import lax

LEAF = 256
K = 64
R = 16
NN = 8
NF = 8
LPD = 64
C1DEV = 8
NLEAF = 2048
NC1 = 256
TOPLEV = 5
N_GX = 4
N_GY = 8


def draw_lists(key, row_total, span, slot_count, self_first):
    row_ids = jnp.arange(row_total, dtype=jnp.int32)[:, None]
    offsets = jax.random.randint(key, (row_total, slot_count), -span, span + 1, dtype=jnp.int32)
    entries = jnp.clip(row_ids + offsets, 0, row_total - 1)
    slot_ids = jnp.arange(slot_count, dtype=jnp.int32)[None, :]
    forward = jnp.where(row_ids + span < row_total, row_ids + span, row_ids - span)
    backward = jnp.where(row_ids >= span, row_ids - span, row_ids + span)
    forward_slot = 1 if self_first else 0
    entries = jnp.where(slot_ids == forward_slot, forward, entries)
    entries = jnp.where(slot_ids == slot_count - 1, backward, entries)
    if self_first:
        entries = jnp.where(slot_ids == 0, row_ids, entries)
    return entries.astype(jnp.int32)


def draw_near_list(key, part):
    return draw_lists(jax.random.fold_in(key, 11), NLEAF, LPD, NN, True)


def draw_far_leaf(key, part):
    return draw_lists(jax.random.fold_in(key, 23), NLEAF, LPD, NF, False)


def draw_far_cluster(key, part):
    return draw_lists(jax.random.fold_in(key, 37), NC1, C1DEV, NF, False)


def set_ends(values, rng, smallest, top_value):
    index_at = [jax.random.randint(jax.random.fold_in(rng, axis), (), 0, length) for axis, length in enumerate(values.shape)]
    longest = values.shape.index(max(values.shape))
    beside = index_at[:longest] + [(index_at[longest] + 1) % values.shape[longest]] + index_at[longest + 1:]
    return values.at[tuple(index_at)].set(smallest).at[tuple(beside)].set(top_value)


def levels(stream_key, shape, pieces, least, largest):
    factor_of, own = 1.0, jax.random.fold_in(stream_key, 6)
    for axis_at, parts in pieces:
        draws = jnp.exp(jax.random.uniform(jax.random.fold_in(own, axis_at), (parts,), jnp.float32, least / len(pieces), largest / len(pieces)))
        factor_of = factor_of * jnp.repeat(draws, shape[axis_at] // parts).reshape([-1 if axis == axis_at else 1 for axis in range(len(shape))])
    return factor_of


def gaussian(rng, shape, scale, most, split=(), kind=jnp.bfloat16):
    drawn = scale * jax.random.normal(rng, shape, jnp.float32)
    if split:
        drawn = drawn * levels(rng, shape, split, -0.22, 0.18)
    return jnp.clip(drawn, -most, most).astype(kind)


def setup_inputs(seed: int = 0) -> dict:
    key_list = jax.random.split(jax.random.key(seed), 14)
    return {
        "points": jnp.clip(1.0 * jax.random.uniform(key_list[0], (NLEAF, 3, LEAF), jnp.float32) ** levels(key_list[0], (NLEAF, 3, LEAF), ((0, 32),), -0.2, 0.2), 0.0, 1.0).astype(jnp.bfloat16),
        "charges": gaussian(key_list[1], (NLEAF, R, LEAF), 1.0, 6.0, ((0, 32),)),
        "near_list": draw_near_list(jax.random.fold_in(key_list[13], 71), 0),
        "near_count": set_ends(jax.random.randint(key_list[3], (NLEAF,), 1, NN + 1), jax.random.fold_in(key_list[3], 1), 1, NN).astype(jnp.int32),
        "far_leaf": draw_far_leaf(jax.random.fold_in(key_list[13], 71), 0),
        "far_cluster": draw_far_cluster(jax.random.fold_in(key_list[13], 71), 0),
        "basis": gaussian(key_list[6], (NLEAF, K, LEAF), LEAF ** -0.5, 0.375, ((0, 32),)),
        "leaf_transfer": gaussian(key_list[7], (NLEAF, K * K), (2 * K) ** -0.5, 0.5, ((0, 32),)),
        "cluster_transfer": gaussian(key_list[8], (NC1, K * K), (2 * K) ** -0.5, 0.5, ((0, 32),)),
        "leaf_coupling": gaussian(key_list[9], (NLEAF, NF, K * K), (NF * K) ** -0.5, 0.25, ((0, 32),)),
        "cluster_coupling": gaussian(key_list[10], (NC1, NF, K * K), (NF * K) ** -0.5, 0.25, ((0, 32),)),
        "top_transfer": gaussian(key_list[11], (2, K, K), (2 * K) ** -0.5, 0.5),
        "top_coupling": gaussian(key_list[12], (2, K, K), K ** -0.5, 0.75),
    }


SOFTENING = 0.0025
STRENGTH = 0.0625
ROOT_TWO = 1.4142135623730951

def kernel_tile(target, source, live):
    squared = jnp.zeros((target.shape[0], target.shape[2], source.shape[2]), jnp.float32)
    for component in range(3):
        spread = target[:, component, :, None].astype(jnp.float32) - source[:, component, None, :].astype(jnp.float32)
        squared = squared + spread * spread
    values = STRENGTH / jnp.sqrt(squared + SOFTENING)
    return jnp.where(live[:, None, None], values, 0.0).astype(jnp.bfloat16)

def level_product(stack_in, matrix):
    return jnp.einsum('nrk,kp->nrp', stack_in.astype(jnp.float32), matrix.astype(jnp.float32))

def reference(points, charges, near_list, near_count, far_leaf, far_cluster, basis, leaf_transfer, cluster_transfer, leaf_coupling, cluster_coupling, top_transfer, top_coupling):
    leaf_total, rhs_count, leaf_size = charges.shape
    rank_size = basis.shape[1]
    device_total = N_GX * N_GY
    moments = jnp.einsum('lrs,lks->lrk', charges.astype(jnp.float32), basis.astype(jnp.float32)).astype(jnp.bfloat16)
    leaf_maps = leaf_transfer.reshape(leaf_total, rank_size, rank_size).astype(jnp.float32)
    raised = jnp.einsum('lrk,lkp->lrp', moments.astype(jnp.float32), leaf_maps)
    parent_mom = raised.reshape(leaf_total // 8, 8, rhs_count, rank_size).sum(axis=1).astype(jnp.bfloat16)
    parent_maps = cluster_transfer.reshape(-1, rank_size, rank_size).astype(jnp.float32)
    device_mom = jnp.einsum('crk,ckp->crp', parent_mom.astype(jnp.float32), parent_maps)
    device_mom = device_mom.reshape(device_total, C1DEV, rhs_count, rank_size).sum(axis=1).astype(jnp.bfloat16)
    upward = []
    current = device_mom
    for height in range(TOPLEV):
        upward.append(current)
        pair_view = current.reshape(-1, 2, rhs_count, rank_size)
        current = (level_product(pair_view[:, 0], top_transfer[0]) + level_product(pair_view[:, 1], top_transfer[1])).astype(jnp.bfloat16)
    local_field = jnp.zeros((1, rhs_count, rank_size), jnp.float32)
    for height in reversed(range(TOPLEV)):
        pair_view = upward[height].reshape(-1, 2, rhs_count, rank_size)
        rounded = local_field.astype(jnp.bfloat16)
        lower_child = level_product(pair_view[:, 1], top_coupling[0]) + ROOT_TWO * level_product(rounded, top_transfer[0].T)
        upper_child = level_product(pair_view[:, 0], top_coupling[1]) + ROOT_TWO * level_product(rounded, top_transfer[1].T)
        local_field = jnp.stack([lower_child, upper_child], axis=1).reshape(-1, rhs_count, rank_size)
    device_local = local_field.astype(jnp.bfloat16)
    parent_coup = cluster_coupling.reshape(-1, NF, rank_size, rank_size).astype(jnp.float32)
    parent_local = jnp.einsum('cfrk,cfkp->crp', parent_mom[far_cluster].astype(jnp.float32), parent_coup)
    spread_local = jnp.repeat(device_local, C1DEV, axis=0).astype(jnp.float32)
    parent_local = (parent_local + jnp.einsum('crp,ckp->crk', spread_local, parent_maps)).astype(jnp.bfloat16)

    def one_block(block_index):
        start = (block_index * LPD).astype(jnp.int32)

        def row_block(source_array):
            return lax.dynamic_slice_in_dim(source_array, start, LPD, 0)
        target = row_block(points)
        near_rows = row_block(near_list)
        used = row_block(near_count)

        def add_slot(slot_index, running):
            source_index = lax.dynamic_index_in_dim(near_rows, slot_index, 1, keepdims=False)
            tile = kernel_tile(target, points[source_index], slot_index < used)
            return running + jnp.einsum('lts,lrs->lrt', tile.astype(jnp.float32), charges[source_index].astype(jnp.float32))
        near_field = lax.fori_loop(0, NN, add_slot, jnp.zeros((LPD, rhs_count, leaf_size), jnp.float32))
        far_rows = row_block(far_leaf)
        leaf_coup = row_block(leaf_coupling).reshape(LPD, NF, rank_size, rank_size).astype(jnp.float32)
        above = jnp.repeat(lax.dynamic_slice_in_dim(parent_local, start // 8, LPD // 8, 0), 8, axis=0)
        leaf_local = jnp.einsum('lfrk,lfkp->lrp', moments[far_rows].astype(jnp.float32), leaf_coup)
        leaf_local = leaf_local + jnp.einsum('lrp,lkp->lrk', above.astype(jnp.float32), row_block(leaf_maps))
        leaf_local = leaf_local.astype(jnp.bfloat16)
        return near_field + jnp.einsum('lrk,lks->lrs', leaf_local.astype(jnp.float32), row_block(basis).astype(jnp.float32))
    result = lax.map(one_block, jnp.arange(leaf_total // LPD, dtype=jnp.int32))
    return result.reshape(leaf_total, rhs_count, leaf_size)
```

```python
import functools

import jax
import jax.numpy as jnp
from jax import lax
from jax.experimental import pallas as pl
from jax.experimental.pallas import tpu as pltpu
from jax.sharding import PartitionSpec as P

SOFTENING = 0.0025
ROOT_TWO = 1.4142135623730951
MESH = pl.DeviceIdType.MESH
F32 = jnp.float32
BF16 = jnp.bfloat16
ROWS = 16


def dot(a, b, left=1, right=0):
    return lax.dot_general(a, b, (((left,), (right,)), ((), ())), preferred_element_type=F32)


def spread_map(parity, rank, links):
    lane = lax.broadcasted_iota(jnp.int32, (rank, rank // 2 * links), 1)
    row = lax.broadcasted_iota(jnp.int32, (rank, rank // 2 * links), 0)
    return jnp.where(row == lane // links * 2 + parity, 1.0, 0.0).astype(BF16)


def link_mask(rows, links, lanes, per_link):
    lane = lax.broadcasted_iota(jnp.int32, (rows, lanes), 1)
    row = lax.broadcasted_iota(jnp.int32, (rows, lanes), 0)
    return jnp.where(lane % links == row // per_link, 1.0, 0.0)


def fold(product, rhs, rank):
    return product[:rhs, :rank] + product[rhs:, rank:]


def gathered_up(stack, maps, mask, links, rhs):
    halves = []
    for spread in maps:
        wide = dot(stack, spread) * mask
        halves.append(wide.reshape(links, rhs, wide.shape[1]).sum(axis=0))
    return jnp.concatenate(halves, axis=0).astype(BF16)


def block_diagonal(value):
    zero = jnp.zeros_like(value)
    upper = jnp.concatenate([value, zero], axis=1)
    lower = jnp.concatenate([zero, value], axis=1)
    return jnp.concatenate([upper, lower], axis=0).astype(BF16)


def spread_down(value, matrix, maps, mask, links, rhs):
    product = dot(block_diagonal(value), matrix, 1, 1)
    total = None
    for parity, spread in enumerate(maps):
        half = product[parity * rhs : (parity + 1) * rhs]
        tall = (jnp.concatenate([half] * links, axis=0) * mask).astype(BF16)
        part = dot(tall, spread, 1, 1)
        total = part if total is None else total + part
    return total


def exchange_kernel(
    grid_shape,
    points,
    charges,
    basis,
    leaf_maps,
    parent_maps,
    top_transfer,
    top_coupling,
    wide_points,
    wide_charges,
    wide_moments,
    wide_parents,
    device_local,
    sent,
    arrived,
    send_sem,
    recv_sem,
    tree_send,
    tree_recv,
    own_sem,
):
    across, along = grid_shape
    total = across * along
    levels = total.bit_length() - 1
    me = lax.axis_index("gx") * along + lax.axis_index("gy")
    leaves, rhs, _ = charges.shape
    rank = basis.shape[1]
    parents = leaf_maps.shape[0]
    links = leaves // parents

    def place(index):
        return (index // along, index % along)

    def sibling(height):
        step = 2**height
        return me + step - 2 * step * ((me // step) % 2)

    barrier = pltpu.get_barrier_semaphore()

    @pl.when(me > 0)
    def _():
        pl.semaphore_signal(barrier, inc=1, device_id=place(me - 1), device_id_type=MESH)

    @pl.when(me < total - 1)
    def _():
        pl.semaphore_signal(barrier, inc=1, device_id=place(me + 1), device_id_type=MESH)

    for height in range(levels):
        pl.semaphore_signal(barrier, inc=1, device_id=place(sibling(height)), device_id_type=MESH)

    own_points = pltpu.make_async_copy(points, wide_points.at[1], own_sem.at[0])
    own_charges = pltpu.make_async_copy(charges, wide_charges.at[1], own_sem.at[1])
    own_points.start()
    own_charges.start()

    group = 4

    def one_moment(step, carry):
        for inner in range(group):
            leaf = step * group + inner
            value = dot(charges[leaf], basis[leaf], 1, 1).astype(BF16)
            wide_moments[1, pl.ds(pl.multiple_of(leaf * rhs, rhs), rhs), :] = value
        return carry

    lax.fori_loop(0, leaves // group, one_moment, 0)
    maps = [spread_map(parity, rank, links) for parity in range(2)]
    mask = link_mask(links * rhs, links, rank // 2 * links, rhs)
    for parent in range(parents):
        stack = wide_moments[1, parent * links * rhs : (parent + 1) * links * rhs, :]
        product = dot(gathered_up(stack, maps, mask, links, rhs), leaf_maps[parent])
        wide_parents[1, parent * rhs : (parent + 1) * rhs, :] = fold(product, rhs, rank).astype(BF16)
    product = dot(gathered_up(wide_parents[1], maps, mask, parents, rhs), parent_maps[...])
    current = fold(product, rhs, rank).astype(BF16)
    sent[0] = current

    pl.semaphore_wait(barrier, levels + jnp.where(me > 0, 1, 0) + jnp.where(me < total - 1, 1, 0))

    sources = (
        (wide_parents.at[1], wide_parents),
        (wide_moments.at[1], wide_moments),
        (points, wide_points),
        (charges, wide_charges),
    )

    def rightward(index):
        source, target = sources[index]
        return pltpu.make_async_remote_copy(
            src_ref=source,
            dst_ref=target.at[0],
            send_sem=send_sem.at[index, 0],
            recv_sem=recv_sem.at[index, 0],
            device_id=place(jnp.minimum(me + 1, total - 1)),
            device_id_type=MESH,
        )

    def leftward(index):
        source, target = sources[index]
        return pltpu.make_async_remote_copy(
            src_ref=source,
            dst_ref=target.at[2],
            send_sem=send_sem.at[index, 1],
            recv_sem=recv_sem.at[index, 1],
            device_id=place(jnp.maximum(me - 1, 0)),
            device_id_type=MESH,
        )

    def climb(height):
        return pltpu.make_async_remote_copy(
            src_ref=sent.at[height],
            dst_ref=arrived.at[height],
            send_sem=tree_send.at[height],
            recv_sem=tree_recv.at[height],
            device_id=place(sibling(height)),
            device_id_type=MESH,
        )

    climb(0).start()

    @pl.when(me < total - 1)
    def _():
        for index in range(len(sources)):
            rightward(index).start()

    @pl.when(me > 0)
    def _():
        for index in range(len(sources)):
            leftward(index).start()

    couplings = []
    sides = []
    for height in range(levels):
        climb(height).wait()
        side = (me // 2**height) % 2
        sides.append(side)
        other = arrived[height]
        couplings.append(dot(other, top_coupling[side]))
        if height < levels - 1:
            raised = dot(sent[height], top_transfer[side]) + dot(other, top_transfer[1 - side])
            sent[height + 1] = raised.astype(BF16)
            climb(height + 1).start()
    field = couplings[levels - 1]
    for height in reversed(range(levels - 1)):
        field = couplings[height] + ROOT_TWO * dot(field.astype(BF16), top_transfer[sides[height]], 1, 1)
    device_local[...] = field.astype(BF16)

    own_points.wait()
    own_charges.wait()

    @pl.when(me < total - 1)
    def _():
        for index in range(len(sources)):
            rightward(index).wait_send()
            leftward(index).wait_recv()

    @pl.when(me > 0)
    def _():
        for index in range(len(sources)):
            leftward(index).wait_send()
            rightward(index).wait_recv()


def local_kernel(
    grid_shape,
    near_list,
    near_count,
    far_leaf,
    far_cluster,
    points,
    charges,
    moments,
    parent_moments,
    device_local,
    leaf_maps,
    parent_maps,
    parent_couplings,
    leaf_couplings_hbm,
    basis_hbm,
    potential,
    leaf_couplings,
    basis,
    target_table,
    source_table,
    moment_table,
    parent_table,
    near,
    far,
    local,
    pair_source,
    pair_target,
    sems,
):
    along = grid_shape[1]
    me = lax.axis_index("gx") * along + lax.axis_index("gy")
    _, leaves, rhs, size = charges.shape
    wide = 3 * leaves
    rank = basis.shape[1]
    parents = leaf_maps.shape[0]
    links = leaves // parents
    slots = near_list.shape[0] // leaves
    get_coupling = pltpu.make_async_copy(leaf_couplings_hbm, leaf_couplings, sems.at[0])
    get_basis = pltpu.make_async_copy(basis_hbm, basis, sems.at[1])
    get_coupling.start()
    get_basis.start()

    shift = leaves - me * leaves

    def list_leaf(leaf, count):
        used = near_count[leaf]
        for slot in range(slots):
            pair_source[count] = near_list[leaf * slots + slot] + shift
            pair_target[count] = leaf
            count = count + jnp.where(slot < used, 1, 0)
        return count

    pairs = lax.fori_loop(0, leaves, list_leaf, 0)
    group = 4
    for extra in range(group):
        pair_source[pairs + extra] = leaves
        pair_target[pairs + extra] = leaves

    zero = jnp.zeros((16, size), F32)
    one = jnp.ones((16, size), F32)
    for block in range(3):
        for start in range(0, leaves, 16):
            at = block * leaves + start
            own = [points[block, axis, start : start + 16, :].astype(F32) for axis in range(3)]
            norm = own[0] * own[0] + own[1] * own[1] + own[2] * own[2]

            def split(value):
                first = value.astype(BF16).astype(F32)
                second = (value - first).astype(BF16).astype(F32)
                return [first, second, value - first - second]

            source_rows = [-512.0 * value for value in own]
            source_rows += [256.0 * value for value in split(norm + SOFTENING)] + [256.0 * one] * 3
            target_rows = own + [one] * 3 + split(norm)
            for row in range(ROWS):
                value = source_rows[row] if row < 9 else zero
                for half in range(size // 128):
                    base = (half * ROWS + row) * wide + at
                    source_table[base : base + 16, :] = value[:, half * 128 : half * 128 + 128]
                if block == 1:
                    value = target_rows[row] if row < 9 else zero
                    for half in range(size // 128):
                        base = (half * ROWS + row) * leaves + start
                        target_table[base : base + 16, :] = value[:, half * 128 : half * 128 + 128]
    near[...] = jnp.zeros_like(near)

    def side_of(table, leaf, stride):
        pieces = [
            table[pl.ds(half * ROWS * stride + leaf, ROWS, stride=stride), :]
            for half in range(size // 128)
        ]
        return jnp.concatenate(pieces, axis=1).astype(BF16)

    def some_pairs(step, carry):
        results = []
        for inner in range(group):
            source = pair_source[step * group + inner]
            target = pair_target[step * group + inner]
            source_side = side_of(source_table, source, wide)
            safe = jnp.minimum(target, leaves - 1)
            target_side = side_of(target_table, safe, leaves)
            squared = dot(source_side, target_side, 0, 0)
            tile = lax.rsqrt(squared).astype(BF16)
            results.append((target, dot(charges[source // leaves, source % leaves], tile)))
        for target, value in results:
            near[target] = near[target] + value
        return carry

    lax.fori_loop(0, (pairs + group - 1) // group, some_pairs, 0)

    maps = [spread_map(parity, rank, links) for parity in range(2)]
    for block in range(3):
        for parity in range(2):
            value = dot(moments[block], maps[parity]).astype(BF16)
            moment_table[
                block * leaves : (block + 1) * leaves, parity * rhs : (parity + 1) * rhs, :
            ] = value.reshape(leaves, rhs, value.shape[1])
            value = dot(parent_moments[block], maps[parity]).astype(BF16)
            parent_table[
                block * parents : (block + 1) * parents, parity * rhs : (parity + 1) * rhs, :
            ] = value.reshape(parents, rhs, value.shape[1])
    lanes = rank // 2 * links
    lane = lax.broadcasted_iota(jnp.int32, (2 * rhs, lanes), 1) % links
    masks = [jnp.where(lane == link, 1.0, 0.0).astype(BF16) for link in range(links)]

    def collect(table, index, row, offset):
        total = None
        for link in range(links):
            part = table[index[row * links + link] + offset] * masks[link]
            total = part if total is None else total + part
        return total

    parent_shift = parents - me * parents
    mask = link_mask(links * rhs, links, lanes, rhs)
    down = spread_down(device_local[...].astype(F32), parent_maps[...], maps, mask, links, rhs)
    parent_local = []
    for parent in range(parents):
        product = dot(collect(parent_table, far_cluster, parent, parent_shift), parent_couplings[parent])
        value = fold(product, rhs, rank) + down[parent * rhs : (parent + 1) * rhs]
        parent_local.append(value.astype(BF16).astype(F32))
    get_coupling.wait()

    def some_leaves(step, carry):
        for inner in range(group):
            leaf = step * group + inner
            product = dot(collect(moment_table, far_leaf, leaf, shift), leaf_couplings[leaf])
            far[pl.ds(pl.multiple_of(leaf * rhs, rhs), rhs), :] = fold(product, rhs, rank)
        return carry

    lax.fori_loop(0, leaves // group, some_leaves, 0)
    for parent in range(parents):
        down = spread_down(parent_local[parent], leaf_maps[parent], maps, mask, links, rhs)
        rows = slice(parent * links * rhs, (parent + 1) * links * rhs)
        local[rows, :] = (far[rows, :] + down).astype(BF16)
    get_basis.wait()

    def finish(step, carry):
        for inner in range(group):
            leaf = step * group + inner
            value = local[pl.ds(pl.multiple_of(leaf * rhs, rhs), rhs), :]
            potential[leaf] = near[leaf] + dot(value, basis[leaf])
        return carry

    lax.fori_loop(0, leaves // group, finish, 0)


def stored(matrix, links):
    length = matrix.shape[-1]
    tiles = length // 128
    value = matrix.reshape(-1, links, tiles, 128).transpose(0, 2, 1, 3)
    return value.reshape(-1, tiles * links, 128)


def on_device(
    grid_shape,
    points,
    charges,
    near_list,
    near_count,
    far_leaf,
    far_cluster,
    basis,
    leaf_transfer,
    cluster_transfer,
    leaf_coupling,
    cluster_coupling,
    top_transfer,
    top_coupling,
):
    leaves, rhs, size = charges.shape
    rank = basis.shape[1]
    parents = cluster_transfer.shape[0]
    links = far_leaf.shape[1]
    levels = (grid_shape[0] * grid_shape[1]).bit_length() - 1
    turned = points.transpose(1, 0, 2)
    leaf_maps = stored(leaf_transfer, links)
    parent_maps = stored(cluster_transfer, links)[0]
    leaf_couplings = stored(leaf_coupling, links)
    parent_couplings = stored(cluster_coupling, links)
    vmem = pl.BlockSpec(memory_space=pltpu.VMEM)
    smem = pl.BlockSpec(memory_space=pltpu.SMEM)
    hbm = pl.BlockSpec(memory_space=pl.ANY)
    shape = jax.ShapeDtypeStruct
    wide_points, wide_charges, moments, parent_moments, device_local = pl.pallas_call(
        functools.partial(exchange_kernel, grid_shape),
        out_shape=(
            shape((3,) + turned.shape, BF16),
            shape((3,) + charges.shape, BF16),
            shape((3, leaves * rhs, rank), BF16),
            shape((3, parents * rhs, rank), BF16),
            shape((rhs, rank), BF16),
        ),
        in_specs=[vmem] * 7,
        out_specs=(hbm, hbm, vmem, vmem, vmem),
        scratch_shapes=[
            pltpu.VMEM((levels, rhs, rank), BF16),
            pltpu.VMEM((levels, rhs, rank), BF16),
            pltpu.SemaphoreType.DMA((4, 2)),
            pltpu.SemaphoreType.DMA((4, 2)),
            pltpu.SemaphoreType.DMA((levels,)),
            pltpu.SemaphoreType.DMA((levels,)),
            pltpu.SemaphoreType.DMA((2,)),
        ],
        compiler_params=pltpu.CompilerParams(
            collective_id=0, has_side_effects=True, vmem_limit_bytes=32 << 20
        ),
        name="exchange",
    )(turned, charges, basis, leaf_maps, parent_maps, top_transfer, top_coupling)
    slots = near_list.shape[1]
    return pl.pallas_call(
        functools.partial(local_kernel, grid_shape),
        out_shape=shape((leaves, rhs, size), F32),
        in_specs=[smem] * 4 + [vmem] * 8 + [hbm] * 2,
        out_specs=vmem,
        scratch_shapes=[
            pltpu.VMEM(leaf_couplings.shape, BF16),
            pltpu.VMEM(basis.shape, BF16),
            pltpu.VMEM((size // 128 * ROWS * leaves, 128), F32),
            pltpu.VMEM((size // 128 * ROWS * 3 * leaves, 128), F32),
            pltpu.VMEM((3 * leaves, 2 * rhs, rank // 2 * links), BF16),
            pltpu.VMEM((3 * parents, 2 * rhs, rank // 2 * links), BF16),
            pltpu.VMEM((leaves + 1, rhs, size), F32),
            pltpu.VMEM((leaves * rhs, rank), F32),
            pltpu.VMEM((leaves * rhs, rank), BF16),
            pltpu.SMEM((leaves * slots + 8,), jnp.int32),
            pltpu.SMEM((leaves * slots + 8,), jnp.int32),
            pltpu.SemaphoreType.DMA((2,)),
        ],
        compiler_params=pltpu.CompilerParams(vmem_limit_bytes=48 << 20),
        name="local",
    )(
        near_list.reshape(-1),
        near_count,
        far_leaf.reshape(-1),
        far_cluster.reshape(-1),
        wide_points,
        wide_charges,
        moments,
        parent_moments,
        device_local,
        leaf_maps,
        parent_maps,
        parent_couplings,
        leaf_couplings,
        basis,
    )


def solution(mesh):
    grid_shape = (mesh.shape["gx"], mesh.shape["gy"])
    both = ("gx", "gy")
    in_specs = (
        P(both, None, None),
        P(both, None, None),
        P(both, None),
        P(both),
        P(both, None),
        P(both, None),
        P(both, None, None),
        P(both, None),
        P(both, None),
        P(both, None, None),
        P(both, None, None),
        P(),
        P(),
    )
    return jax.shard_map(
        functools.partial(on_device, grid_shape),
        mesh=mesh,
        in_specs=in_specs,
        out_specs=P(both, None, None),
        check_vma=False,
    )
```

```python
import functools

import jax
import jax.numpy as jnp
from jax import lax
from jax.experimental import pallas as pl
from jax.experimental.pallas import tpu as pltpu
from jax.sharding import PartitionSpec as P

SOFTENING = 0.0025
ROOT_TWO = 1.4142135623730951
MESH = pl.DeviceIdType.MESH
F32 = jnp.float32
BF16 = jnp.bfloat16
ROWS = 16
EARLY = 2
GROUP = 16


def dot(a, b, left=1, right=0):
    return lax.dot_general(a, b, (((left,), (right,)), ((), ())), preferred_element_type=F32)


def spread_map(parity, rank, links):
    lane = lax.broadcasted_iota(jnp.int32, (rank, rank // 2 * links), 1)
    row = lax.broadcasted_iota(jnp.int32, (rank, rank // 2 * links), 0)
    return jnp.where(row == lane // links * 2 + parity, 1.0, 0.0).astype(BF16)


def link_mask(rows, links, lanes, per_link):
    lane = lax.broadcasted_iota(jnp.int32, (rows, lanes), 1)
    row = lax.broadcasted_iota(jnp.int32, (rows, lanes), 0)
    return jnp.where(lane % links == row // per_link, 1.0, 0.0)


def fold(product, rhs, rank):
    return product[:rhs, :rank] + product[rhs:, rank:]


def gathered_up(stack, maps, mask, links, rhs):
    halves = []
    for spread in maps:
        wide = dot(stack, spread) * mask
        halves.append(wide.reshape(links, rhs, wide.shape[1]).sum(axis=0))
    return jnp.concatenate(halves, axis=0).astype(BF16)


def block_diagonal(value):
    zero = jnp.zeros_like(value)
    upper = jnp.concatenate([value, zero], axis=1)
    lower = jnp.concatenate([zero, value], axis=1)
    return jnp.concatenate([upper, lower], axis=0).astype(BF16)


def spread_down(value, matrix, maps, mask, links, rhs):
    product = dot(block_diagonal(value), matrix, 1, 1)
    total = None
    for parity, spread in enumerate(maps):
        half = product[parity * rhs : (parity + 1) * rhs]
        tall = (jnp.concatenate([half] * links, axis=0) * mask).astype(BF16)
        part = dot(tall, spread, 1, 1)
        total = part if total is None else total + part
    return total


def split(value):
    first = value.astype(BF16).astype(F32)
    second = (value - first).astype(BF16).astype(F32)
    return [first, second, value - first - second]


def augmented(coordinates):
    one = jnp.ones_like(coordinates[0])
    norm = sum(value * value for value in coordinates)
    source = [-512.0 * value for value in coordinates]
    source += [256.0 * value for value in split(norm + SOFTENING)] + [256.0 * one] * 3
    target = coordinates + [one] * 3 + split(norm)
    zero = [jnp.zeros_like(one)] * (ROWS - len(source))
    return source + zero, target + zero


def put_rows(table, rows, at, stride):
    for row, value in enumerate(rows):
        for half in range(value.shape[1] // 128):
            base = (half * ROWS + row) * stride + at
            table[base : base + 16, :] = value[:, half * 128 : half * 128 + 128]


def side_of(table, leaf, stride):
    halves = table.shape[0] // (ROWS * stride)
    pieces = [
        table[pl.ds(half * ROWS * stride + leaf, ROWS, stride=stride), :] for half in range(halves)
    ]
    return jnp.concatenate(pieces, axis=1).astype(BF16)


def near_tile(target_side, source_side):
    return lax.rsqrt(dot(target_side, source_side, 0, 0)).astype(BF16)


def exchange_kernel(
    grid_shape,
    near_list,
    near_count,
    far_leaf,
    far_cluster,
    top_transfer,
    top_coupling,
    points_hbm,
    charges_hbm,
    basis_hbm,
    leaf_maps_hbm,
    parent_maps_hbm,
    parent_couplings_hbm,
    leaf_couplings_hbm,
    wide_points,
    wide_charges,
    partial,
    wide_moments,
    wide_parents,
    own_charges,
    basis,
    leaf_maps,
    parent_maps,
    parent_couplings,
    leaf_couplings,
    target_table,
    source_table,
    target_sides,
    source_sides,
    moment_table,
    parent_table,
    far,
    local,
    sent,
    arrived,
    send_sem,
    recv_sem,
    tree_send,
    tree_recv,
    own_sem,
):
    across, along = grid_shape
    total = across * along
    levels = total.bit_length() - 1
    me = lax.axis_index("gx") * along + lax.axis_index("gy")
    _, leaves, rhs, size = wide_charges.shape
    rank = basis.shape[1]
    parents = leaf_maps.shape[0]
    links = leaves // parents
    slots = near_list.shape[0] // leaves

    def place(index):
        return (index // along, index % along)

    def sibling(height):
        step = 2**height
        return me + step - 2 * step * ((me // step) % 2)

    barrier = pltpu.get_barrier_semaphore()

    @pl.when(me > 0)
    def _():
        pl.semaphore_signal(barrier, inc=1, device_id=place(me - 1), device_id_type=MESH)

    @pl.when(me < total - 1)
    def _():
        pl.semaphore_signal(barrier, inc=1, device_id=place(me + 1), device_id_type=MESH)

    for height in range(levels):
        pl.semaphore_signal(barrier, inc=1, device_id=place(sibling(height)), device_id_type=MESH)

    own = [
        pltpu.make_async_copy(source, target, own_sem.at[index])
        for index, (source, target) in enumerate(
            (
                (points_hbm, wide_points.at[1]),
                (charges_hbm, own_charges),
                (basis_hbm, basis),
                (leaf_maps_hbm, leaf_maps),
                (parent_maps_hbm, parent_maps),
                (parent_couplings_hbm, parent_couplings),
                (leaf_couplings_hbm, leaf_couplings),
                (charges_hbm, wide_charges.at[1]),
            )
        )
    ]
    for copy in own:
        copy.start()
    maps = [spread_map(parity, rank, links) for parity in range(2)]
    lanes = rank // 2 * links
    mask = link_mask(links * rhs, links, lanes, rhs)
    lane = lax.broadcasted_iota(jnp.int32, (2 * rhs, lanes), 1) % links
    masks = [jnp.where(lane == link, 1.0, 0.0).astype(BF16) for link in range(links)]

    arrays = (wide_charges, wide_points, wide_parents, wide_moments)
    mine = (own_charges, wide_points.at[1], wide_parents.at[1], wide_moments.at[1])

    def rightward(index):
        return pltpu.make_async_remote_copy(
            src_ref=mine[index],
            dst_ref=arrays[index].at[0],
            send_sem=send_sem.at[index, 0],
            recv_sem=recv_sem.at[index, 0],
            device_id=place(jnp.minimum(me + 1, total - 1)),
            device_id_type=MESH,
        )

    def leftward(index):
        return pltpu.make_async_remote_copy(
            src_ref=mine[index],
            dst_ref=arrays[index].at[2],
            send_sem=send_sem.at[index, 1],
            recv_sem=recv_sem.at[index, 1],
            device_id=place(jnp.maximum(me - 1, 0)),
            device_id_type=MESH,
        )

    def climb(height):
        return pltpu.make_async_remote_copy(
            src_ref=sent.at[height],
            dst_ref=arrived.at[height],
            send_sem=tree_send.at[height],
            recv_sem=tree_recv.at[height],
            device_id=place(sibling(height)),
            device_id_type=MESH,
        )

    def send(indices):
        @pl.when(me < total - 1)
        def _():
            for index in indices:
                rightward(index).start()

        @pl.when(me > 0)
        def _():
            for index in indices:
                leftward(index).start()

    def settle(indices):
        @pl.when(me < total - 1)
        def _():
            for index in indices:
                rightward(index).wait_send()
                leftward(index).wait_recv()

        @pl.when(me > 0)
        def _():
            for index in indices:
                leftward(index).wait_send()
                rightward(index).wait_recv()

    own[0].wait()
    own[1].wait()
    pl.semaphore_wait(barrier, levels + jnp.where(me > 0, 1, 0) + jnp.where(me < total - 1, 1, 0))
    send((0, 1))
    own[2].wait()
    group = 8

    def one_moment(step, carry):
        for inner in range(group):
            leaf = step * group + inner
            value = dot(own_charges[leaf], basis[leaf], 1, 1).astype(BF16)
            wide_moments[1, pl.ds(pl.multiple_of(leaf * rhs, rhs), rhs), :] = value
        return carry

    lax.fori_loop(0, leaves // group, one_moment, 0)
    own[3].wait()
    for parent in range(parents):
        stack = wide_moments[1, parent * links * rhs : (parent + 1) * links * rhs, :]
        product = dot(gathered_up(stack, maps, mask, links, rhs), leaf_maps[parent])
        wide_parents[1, parent * rhs : (parent + 1) * rhs, :] = fold(product, rhs, rank).astype(BF16)
    own[4].wait()
    product = dot(gathered_up(wide_parents[1], maps, mask, parents, rhs), parent_maps[...])
    sent[0] = fold(product, rhs, rank).astype(BF16)
    climb(0).start()
    send((2, 3))

    @pl.when(me == 0)
    def _():
        wide_moments[0] = jnp.zeros(wide_moments.shape[1:], BF16)
        wide_parents[0] = jnp.zeros(wide_parents.shape[1:], BF16)

    @pl.when(me == total - 1)
    def _():
        wide_moments[2] = jnp.zeros(wide_moments.shape[1:], BF16)
        wide_parents[2] = jnp.zeros(wide_parents.shape[1:], BF16)

    for start in range(0, leaves, 16):
        coordinates = [wide_points[1, axis, start : start + 16, :].astype(F32) for axis in range(3)]
        source_rows, target_rows = augmented(coordinates)
        put_rows(source_table, source_rows, start, leaves)
        put_rows(target_table, target_rows, start, leaves)

    def one_side(step, carry):
        for inner in range(group):
            leaf = step * group + inner
            source_sides[leaf] = side_of(source_table, leaf, leaves)
            target_sides[leaf] = side_of(target_table, leaf, leaves)
        return carry

    lax.fori_loop(0, leaves // group, one_side, 0)
    shift = leaves - me * leaves
    batch = 8

    def own_near(step, carry):
        results = []
        for inner in range(batch):
            leaf = step * batch + inner
            used = near_count[leaf]
            rank_of = 0
            found = [0] * EARLY
            for slot in range(slots):
                source = near_list[leaf * slots + slot] - me * leaves
                inside = (source >= 0) & (source < leaves) & (slot < used)
                for place_at in range(EARLY):
                    found[place_at] = jnp.where(inside & (rank_of == place_at), source, found[place_at])
                rank_of = rank_of + jnp.where(inside, 1, 0)
            tiles = []
            values = []
            for place_at in range(EARLY):
                source = found[place_at]
                tiles.append(near_tile(target_sides[leaf], source_sides[source]))
                weight = jnp.where(rank_of > place_at, 1.0, 0.0).astype(F32)
                values.append((own_charges[source].astype(F32) * weight).astype(BF16))
            wide_tile = jnp.concatenate(tiles, axis=1)
            wide_value = jnp.concatenate(values, axis=1)
            results.append(dot(wide_tile, wide_value, 1, 1).T)
        for inner in range(batch):
            partial[step * batch + inner] = results[inner]
        return carry

    couplings = []
    sides = []
    steps = leaves // batch
    for height in range(levels):
        lax.fori_loop(steps * height // levels, steps * (height + 1) // levels, own_near, 0)
        climb(height).wait()
        side = (me // 2**height) % 2
        sides.append(side)
        other = arrived[height]
        couplings.append(dot(other, top_coupling[side]))
        if height < levels - 1:
            raised = dot(sent[height], top_transfer[side]) + dot(other, top_transfer[1 - side])
            sent[height + 1] = raised.astype(BF16)
            climb(height + 1).start()
    field = couplings[levels - 1]
    for height in reversed(range(levels - 1)):
        field = couplings[height] + ROOT_TWO * dot(field.astype(BF16), top_transfer[sides[height]], 1, 1)
    device_local = field.astype(BF16).astype(F32)

    settle((2, 3))
    for block in range(3):
        for parity in range(2):
            value = dot(wide_moments[block], maps[parity]).astype(BF16)
            moment_table[
                block * leaves : (block + 1) * leaves, parity * rhs : (parity + 1) * rhs, :
            ] = value.reshape(leaves, rhs, value.shape[1])
            value = dot(wide_parents[block], maps[parity]).astype(BF16)
            parent_table[
                block * parents : (block + 1) * parents, parity * rhs : (parity + 1) * rhs, :
            ] = value.reshape(parents, rhs, value.shape[1])

    def collect(table, index, row, offset):
        gathered = None
        for link in range(links):
            at = jnp.clip(index[row * links + link] + offset, 0, table.shape[0] - 1)
            part = table[at] * masks[link]
            gathered = part if gathered is None else gathered + part
        return gathered

    own[5].wait()
    parent_shift = parents - me * parents
    down = spread_down(device_local, parent_maps[...], maps, mask, links, rhs)
    parent_local = []
    for parent in range(parents):
        product = dot(collect(parent_table, far_cluster, parent, parent_shift), parent_couplings[parent])
        value = fold(product, rhs, rank) + down[parent * rhs : (parent + 1) * rhs]
        parent_local.append(value.astype(BF16).astype(F32))
    own[6].wait()

    def some_leaves(step, carry):
        for inner in range(group):
            leaf = step * group + inner
            product = dot(collect(moment_table, far_leaf, leaf, shift), leaf_couplings[leaf])
            far[pl.ds(pl.multiple_of(leaf * rhs, rhs), rhs), :] = fold(product, rhs, rank)
        return carry

    lax.fori_loop(0, leaves // group, some_leaves, 0)
    for parent in range(parents):
        down = spread_down(parent_local[parent], leaf_maps[parent], maps, mask, links, rhs)
        rows = slice(parent * links * rhs, (parent + 1) * links * rhs)
        local[rows, :] = (far[rows, :] + down).astype(BF16)

    def finish(step, carry):
        for inner in range(group):
            leaf = step * group + inner
            value = local[pl.ds(pl.multiple_of(leaf * rhs, rhs), rhs), :]
            partial[leaf] = partial[leaf] + dot(value, basis[leaf])
        return carry

    lax.fori_loop(0, leaves // group, finish, 0)
    own[7].wait()
    settle((0, 1))


def near_kernel(
    grid_shape,
    near_list,
    near_count,
    points,
    charges,
    partial,
    potential,
    target_table,
    source_table,
    pair_source,
    pair_target,
):
    along = grid_shape[1]
    me = lax.axis_index("gx") * along + lax.axis_index("gy")
    _, leaves, rhs, size = charges.shape
    wide = 3 * leaves
    slots = near_list.shape[0] // leaves
    shift = leaves - me * leaves
    group = GROUP

    def list_leaf(leaf, count):
        used = near_count[leaf]
        rank_of = 0
        for slot in range(slots):
            source = near_list[leaf * slots + slot] + shift
            live = slot < used
            inside = (source >= leaves) & (source < 2 * leaves) & live
            done = inside & (rank_of < EARLY)
            pair_source[count] = source
            pair_target[count] = leaf
            count = count + jnp.where(live & jnp.logical_not(done), 1, 0)
            rank_of = rank_of + jnp.where(inside, 1, 0)
        return count

    pairs = lax.fori_loop(0, leaves, list_leaf, 0)
    for extra in range(group):
        pair_source[pairs + extra] = leaves
        pair_target[pairs + extra] = 0

    for block in range(3):
        for start in range(0, leaves, 16):
            coordinates = [points[block, axis, start : start + 16, :].astype(F32) for axis in range(3)]
            source_rows, target_rows = augmented(coordinates)
            put_rows(source_table, source_rows, block * leaves + start, wide)
            if block == 1:
                put_rows(target_table, target_rows, start, leaves)
    potential[...] = partial[...]

    def some_pairs(step, carry):
        results = []
        for inner in range(group):
            at = step * group + inner
            source = pair_source[at]
            target = pair_target[at]
            tile = near_tile(side_of(target_table, target, leaves), side_of(source_table, source, wide))
            value = dot(tile, charges[source // leaves, source % leaves], 1, 1).T
            results.append((target, jnp.where(at < pairs, value, 0.0)))
        for target, value in results:
            potential[target] = potential[target] + value
        return carry

    lax.fori_loop(0, (pairs + group - 1) // group, some_pairs, 0)


def stored(matrix, links):
    length = matrix.shape[-1]
    tiles = length // 128
    value = matrix.reshape(-1, links, tiles, 128).transpose(0, 2, 1, 3)
    return value.reshape(-1, tiles * links, 128)


def on_device(
    grid_shape,
    points,
    charges,
    near_list,
    near_count,
    far_leaf,
    far_cluster,
    basis,
    leaf_transfer,
    cluster_transfer,
    leaf_coupling,
    cluster_coupling,
    top_transfer,
    top_coupling,
):
    leaves, rhs, size = charges.shape
    rank = basis.shape[1]
    parents = cluster_transfer.shape[0]
    links = far_leaf.shape[1]
    levels = (grid_shape[0] * grid_shape[1]).bit_length() - 1
    turned = points.transpose(1, 0, 2)
    leaf_maps = stored(leaf_transfer, links)
    parent_maps = stored(cluster_transfer, links)[0]
    leaf_couplings = stored(leaf_coupling, links)
    parent_couplings = stored(cluster_coupling, links)
    vmem = pl.BlockSpec(memory_space=pltpu.VMEM)
    smem = pl.BlockSpec(memory_space=pltpu.SMEM)
    hbm = pl.BlockSpec(memory_space=pl.ANY)
    shape = jax.ShapeDtypeStruct
    near_flat = near_list.reshape(-1)
    slots = near_list.shape[1]
    spread = rank // 2 * links
    halves = size // 128
    wide_points, wide_charges, partial = pl.pallas_call(
        functools.partial(exchange_kernel, grid_shape),
        out_shape=(
            shape((3,) + turned.shape, BF16),
            shape((3,) + charges.shape, BF16),
            shape((leaves, rhs, size), F32),
        ),
        in_specs=[smem] * 4 + [vmem] * 2 + [hbm] * 7,
        out_specs=(vmem, vmem, vmem),
        scratch_shapes=[
            pltpu.VMEM((3, leaves * rhs, rank), BF16),
            pltpu.VMEM((3, parents * rhs, rank), BF16),
            pltpu.VMEM(charges.shape, BF16),
            pltpu.VMEM(basis.shape, BF16),
            pltpu.VMEM(leaf_maps.shape, BF16),
            pltpu.VMEM(parent_maps.shape, BF16),
            pltpu.VMEM(parent_couplings.shape, BF16),
            pltpu.VMEM(leaf_couplings.shape, BF16),
            pltpu.VMEM((halves * ROWS * leaves, 128), F32),
            pltpu.VMEM((halves * ROWS * leaves, 128), F32),
            pltpu.VMEM((leaves, ROWS, size), BF16),
            pltpu.VMEM((leaves, ROWS, size), BF16),
            pltpu.VMEM((3 * leaves, 2 * rhs, spread), BF16),
            pltpu.VMEM((3 * parents, 2 * rhs, spread), BF16),
            pltpu.VMEM((leaves * rhs, rank), F32),
            pltpu.VMEM((leaves * rhs, rank), BF16),
            pltpu.VMEM((levels, rhs, rank), BF16),
            pltpu.VMEM((levels, rhs, rank), BF16),
            pltpu.SemaphoreType.DMA((4, 2)),
            pltpu.SemaphoreType.DMA((4, 2)),
            pltpu.SemaphoreType.DMA((levels,)),
            pltpu.SemaphoreType.DMA((levels,)),
            pltpu.SemaphoreType.DMA((8,)),
        ],
        compiler_params=pltpu.CompilerParams(
            collective_id=0, has_side_effects=True, vmem_limit_bytes=48 << 20
        ),
        name="exchange",
    )(
        near_flat,
        near_count,
        far_leaf.reshape(-1),
        far_cluster.reshape(-1),
        top_transfer,
        top_coupling,
        turned,
        charges,
        basis,
        leaf_maps,
        parent_maps,
        parent_couplings,
        leaf_couplings,
    )
    return pl.pallas_call(
        functools.partial(near_kernel, grid_shape),
        out_shape=shape((leaves, rhs, size), F32),
        in_specs=[smem] * 2 + [vmem] * 3,
        out_specs=vmem,
        scratch_shapes=[
            pltpu.VMEM((halves * ROWS * leaves, 128), F32),
            pltpu.VMEM((halves * ROWS * 3 * leaves, 128), F32),
            pltpu.SMEM((leaves * slots + GROUP,), jnp.int32),
            pltpu.SMEM((leaves * slots + GROUP,), jnp.int32),
        ],
        compiler_params=pltpu.CompilerParams(vmem_limit_bytes=40 << 20),
        name="near",
    )(near_flat, near_count, wide_points, wide_charges, partial)


def solution(mesh):
    grid_shape = (mesh.shape["gx"], mesh.shape["gy"])
    both = ("gx", "gy")
    in_specs = (
        P(both, None, None),
        P(both, None, None),
        P(both, None),
        P(both),
        P(both, None),
        P(both, None),
        P(both, None, None),
        P(both, None),
        P(both, None),
        P(both, None, None),
        P(both, None, None),
        P(),
        P(),
    )
    return jax.shard_map(
        functools.partial(on_device, grid_shape),
        mesh=mesh,
        in_specs=in_specs,
        out_specs=P(both, None, None),
        check_vma=False,
    )
```

```python
import functools

import jax
import jax.numpy as jnp
from jax import lax
from jax.experimental import pallas as pl
from jax.experimental.pallas import tpu as pltpu
from jax.sharding import PartitionSpec as P

SOFTENING = 0.0025
ROOT_TWO = 1.4142135623730951
MESH = pl.DeviceIdType.MESH
F32 = jnp.float32
BF16 = jnp.bfloat16
ROWS = 16
EARLY = 2
GROUP = 16


def dot(a, b, left=1, right=0):
    return lax.dot_general(a, b, (((left,), (right,)), ((), ())), preferred_element_type=F32)


def spread_map(parity, rank, links):
    lane = lax.broadcasted_iota(jnp.int32, (rank, rank // 2 * links), 1)
    row = lax.broadcasted_iota(jnp.int32, (rank, rank // 2 * links), 0)
    return jnp.where(row == lane // links * 2 + parity, 1.0, 0.0).astype(BF16)


def link_mask(rows, links, lanes, per_link):
    lane = lax.broadcasted_iota(jnp.int32, (rows, lanes), 1)
    row = lax.broadcasted_iota(jnp.int32, (rows, lanes), 0)
    return jnp.where(lane % links == row // per_link, 1.0, 0.0)


def fold(product, rhs, rank):
    return product[:rhs, :rank] + product[rhs:, rank:]


def gathered_up(stack, maps, mask, links, rhs):
    halves = []
    for spread in maps:
        wide = dot(stack, spread) * mask
        halves.append(wide.reshape(links, rhs, wide.shape[1]).sum(axis=0))
    return jnp.concatenate(halves, axis=0).astype(BF16)


def block_diagonal(value):
    zero = jnp.zeros_like(value)
    upper = jnp.concatenate([value, zero], axis=1)
    lower = jnp.concatenate([zero, value], axis=1)
    return jnp.concatenate([upper, lower], axis=0).astype(BF16)


def spread_down(value, matrix, maps, mask, links, rhs):
    product = dot(block_diagonal(value), matrix, 1, 1)
    total = None
    for parity, spread in enumerate(maps):
        half = product[parity * rhs : (parity + 1) * rhs]
        tall = (jnp.concatenate([half] * links, axis=0) * mask).astype(BF16)
        part = dot(tall, spread, 1, 1)
        total = part if total is None else total + part
    return total


def split(value):
    first = value.astype(BF16).astype(F32)
    second = (value - first).astype(BF16).astype(F32)
    return [first, second, value - first - second]


def augmented(coordinates):
    one = jnp.ones_like(coordinates[0])
    norm = sum(value * value for value in coordinates)
    source = [-512.0 * value for value in coordinates]
    source += [256.0 * value for value in split(norm + SOFTENING)] + [256.0 * one] * 3
    target = coordinates + [one] * 3 + split(norm)
    zero = [jnp.zeros_like(one)] * (ROWS - len(source))
    return source + zero, target + zero


def put_rows(table, rows, at, stride):
    for row, value in enumerate(rows):
        for half in range(value.shape[1] // 128):
            base = (half * ROWS + row) * stride + at
            table[base : base + 16, :] = value[:, half * 128 : half * 128 + 128]


def side_of(table, leaf, stride):
    halves = table.shape[0] // (ROWS * stride)
    pieces = [
        table[pl.ds(half * ROWS * stride + leaf, ROWS, stride=stride), :] for half in range(halves)
    ]
    return jnp.concatenate(pieces, axis=1).astype(BF16)


def near_tile(target_side, source_side):
    return lax.rsqrt(dot(target_side, source_side, 0, 0)).astype(BF16)


def exchange_kernel(
    grid_shape,
    near_list,
    near_count,
    far_leaf,
    far_cluster,
    top_transfer,
    top_coupling,
    points_hbm,
    charges_hbm,
    basis_hbm,
    leaf_maps_hbm,
    parent_maps_hbm,
    parent_couplings_hbm,
    leaf_couplings_hbm,
    wide_points,
    wide_charges,
    partial,
    wide_moments,
    wide_parents,
    own_charges,
    basis,
    leaf_maps,
    parent_maps,
    parent_couplings,
    leaf_couplings,
    target_table,
    source_table,
    target_sides,
    source_sides,
    moment_table,
    parent_table,
    far,
    local,
    sent,
    arrived,
    send_sem,
    recv_sem,
    tree_send,
    tree_recv,
    own_sem,
):
    across, along = grid_shape
    total = across * along
    levels = total.bit_length() - 1
    me = lax.axis_index("gx") * along + lax.axis_index("gy")
    _, leaves, rhs, size = wide_charges.shape
    rank = basis.shape[1]
    parents = leaf_maps.shape[0]
    links = leaves // parents
    slots = near_list.shape[0] // leaves

    def place(index):
        return (index // along, index % along)

    def sibling(height):
        step = 2**height
        return me + step - 2 * step * ((me // step) % 2)

    barrier = pltpu.get_barrier_semaphore()

    @pl.when(me > 0)
    def _():
        pl.semaphore_signal(barrier, inc=1, device_id=place(me - 1), device_id_type=MESH)

    @pl.when(me < total - 1)
    def _():
        pl.semaphore_signal(barrier, inc=1, device_id=place(me + 1), device_id_type=MESH)

    for height in range(levels):
        pl.semaphore_signal(barrier, inc=1, device_id=place(sibling(height)), device_id_type=MESH)

    own = [
        pltpu.make_async_copy(source, target, own_sem.at[index])
        for index, (source, target) in enumerate(
            (
                (points_hbm, wide_points.at[1]),
                (charges_hbm, own_charges),
                (basis_hbm, basis),
                (leaf_maps_hbm, leaf_maps),
                (parent_maps_hbm, parent_maps),
                (parent_couplings_hbm, parent_couplings),
                (leaf_couplings_hbm, leaf_couplings),
                (charges_hbm, wide_charges.at[1]),
            )
        )
    ]
    for copy in own:
        copy.start()
    maps = [spread_map(parity, rank, links) for parity in range(2)]
    lanes = rank // 2 * links
    mask = link_mask(links * rhs, links, lanes, rhs)
    lane = lax.broadcasted_iota(jnp.int32, (2 * rhs, lanes), 1) % links
    masks = [jnp.where(lane == link, 1.0, 0.0).astype(BF16) for link in range(links)]

    arrays = (wide_charges, wide_points, wide_parents, wide_moments)
    mine = (own_charges, wide_points.at[1], wide_parents.at[1], wide_moments.at[1])

    def rightward(index):
        return pltpu.make_async_remote_copy(
            src_ref=mine[index],
            dst_ref=arrays[index].at[0],
            send_sem=send_sem.at[index, 0],
            recv_sem=recv_sem.at[index, 0],
            device_id=place(jnp.minimum(me + 1, total - 1)),
            device_id_type=MESH,
        )

    def leftward(index):
        return pltpu.make_async_remote_copy(
            src_ref=mine[index],
            dst_ref=arrays[index].at[2],
            send_sem=send_sem.at[index, 1],
            recv_sem=recv_sem.at[index, 1],
            device_id=place(jnp.maximum(me - 1, 0)),
            device_id_type=MESH,
        )

    def climb(height):
        return pltpu.make_async_remote_copy(
            src_ref=sent.at[height],
            dst_ref=arrived.at[height],
            send_sem=tree_send.at[height],
            recv_sem=tree_recv.at[height],
            device_id=place(sibling(height)),
            device_id_type=MESH,
        )

    def send(indices):
        @pl.when(me < total - 1)
        def _():
            for index in indices:
                rightward(index).start()

        @pl.when(me > 0)
        def _():
            for index in indices:
                leftward(index).start()

    def settle(indices):
        @pl.when(me < total - 1)
        def _():
            for index in indices:
                rightward(index).wait_send()
                leftward(index).wait_recv()

        @pl.when(me > 0)
        def _():
            for index in indices:
                leftward(index).wait_send()
                rightward(index).wait_recv()

    own[0].wait()
    own[1].wait()
    pl.semaphore_wait(barrier, levels + jnp.where(me > 0, 1, 0) + jnp.where(me < total - 1, 1, 0))
    own[2].wait()
    group = 8

    def one_moment(step, carry):
        for inner in range(group):
            leaf = step * group + inner
            value = dot(own_charges[leaf], basis[leaf], 1, 1).astype(BF16)
            wide_moments[1, pl.ds(pl.multiple_of(leaf * rhs, rhs), rhs), :] = value
        return carry

    lax.fori_loop(0, leaves // group, one_moment, 0)
    own[3].wait()
    for parent in range(parents):
        stack = wide_moments[1, parent * links * rhs : (parent + 1) * links * rhs, :]
        product = dot(gathered_up(stack, maps, mask, links, rhs), leaf_maps[parent])
        wide_parents[1, parent * rhs : (parent + 1) * rhs, :] = fold(product, rhs, rank).astype(BF16)
    own[4].wait()
    product = dot(gathered_up(wide_parents[1], maps, mask, parents, rhs), parent_maps[...])
    sent[0] = fold(product, rhs, rank).astype(BF16)
    climb(0).start()
    send((2, 3))
    send((0, 1))

    @pl.when(me == 0)
    def _():
        wide_moments[0] = jnp.zeros(wide_moments.shape[1:], BF16)
        wide_parents[0] = jnp.zeros(wide_parents.shape[1:], BF16)

    @pl.when(me == total - 1)
    def _():
        wide_moments[2] = jnp.zeros(wide_moments.shape[1:], BF16)
        wide_parents[2] = jnp.zeros(wide_parents.shape[1:], BF16)

    for start in range(0, leaves, 16):
        coordinates = [wide_points[1, axis, start : start + 16, :].astype(F32) for axis in range(3)]
        source_rows, target_rows = augmented(coordinates)
        put_rows(source_table, source_rows, start, leaves)
        put_rows(target_table, target_rows, start, leaves)

    def one_side(step, carry):
        for inner in range(group):
            leaf = step * group + inner
            source_sides[leaf] = side_of(source_table, leaf, leaves)
            target_sides[leaf] = side_of(target_table, leaf, leaves)
        return carry

    lax.fori_loop(0, leaves // group, one_side, 0)
    shift = leaves - me * leaves
    batch = 8

    def own_near(step, carry):
        results = []
        for inner in range(batch):
            leaf = step * batch + inner
            used = near_count[leaf]
            rank_of = 0
            found = [0] * EARLY
            for slot in range(slots):
                source = near_list[leaf * slots + slot] - me * leaves
                inside = (source >= 0) & (source < leaves) & (slot < used)
                for place_at in range(EARLY):
                    found[place_at] = jnp.where(inside & (rank_of == place_at), source, found[place_at])
                rank_of = rank_of + jnp.where(inside, 1, 0)
            tiles = []
            values = []
            for place_at in range(EARLY):
                source = found[place_at]
                tiles.append(near_tile(target_sides[leaf], source_sides[source]))
                weight = jnp.where(rank_of > place_at, 1.0, 0.0).astype(F32)
                values.append((own_charges[source].astype(F32) * weight).astype(BF16))
            wide_tile = jnp.concatenate(tiles, axis=1)
            wide_value = jnp.concatenate(values, axis=1)
            results.append(dot(wide_tile, wide_value, 1, 1).T)
        for inner in range(batch):
            partial[step * batch + inner] = results[inner]
        return carry

    def collect(table, index, row, offset):
        gathered = None
        for link in range(links):
            at = jnp.clip(index[row * links + link] + offset, 0, table.shape[0] - 1)
            part = table[at] * masks[link]
            gathered = part if gathered is None else gathered + part
        return gathered

    def far_leaves():
        settle((2, 3))
        for block in range(3):
            for parity in range(2):
                value = dot(wide_moments[block], maps[parity]).astype(BF16)
                moment_table[
                    block * leaves : (block + 1) * leaves, parity * rhs : (parity + 1) * rhs, :
                ] = value.reshape(leaves, rhs, value.shape[1])
                value = dot(wide_parents[block], maps[parity]).astype(BF16)
                parent_table[
                    block * parents : (block + 1) * parents, parity * rhs : (parity + 1) * rhs, :
                ] = value.reshape(parents, rhs, value.shape[1])

        own[6].wait()

        def some_leaves(step, carry):
            for inner in range(group):
                leaf = step * group + inner
                product = dot(collect(moment_table, far_leaf, leaf, shift), leaf_couplings[leaf])
                far[pl.ds(pl.multiple_of(leaf * rhs, rhs), rhs), :] = fold(product, rhs, rank)
            return carry

        lax.fori_loop(0, leaves // group, some_leaves, 0)

    couplings = []
    sides = []
    steps = leaves // batch
    for height in range(levels):
        lax.fori_loop(steps * height // levels, steps * (height + 1) // levels, own_near, 0)
        if height == levels // 2:
            far_leaves()
        climb(height).wait()
        side = (me // 2**height) % 2
        sides.append(side)
        other = arrived[height]
        couplings.append(dot(other, top_coupling[side]))
        if height < levels - 1:
            raised = dot(sent[height], top_transfer[side]) + dot(other, top_transfer[1 - side])
            sent[height + 1] = raised.astype(BF16)
            climb(height + 1).start()
    field = couplings[levels - 1]
    for height in reversed(range(levels - 1)):
        field = couplings[height] + ROOT_TWO * dot(field.astype(BF16), top_transfer[sides[height]], 1, 1)
    device_local = field.astype(BF16).astype(F32)

    own[5].wait()
    parent_shift = parents - me * parents
    down = spread_down(device_local, parent_maps[...], maps, mask, links, rhs)
    parent_local = []
    for parent in range(parents):
        product = dot(collect(parent_table, far_cluster, parent, parent_shift), parent_couplings[parent])
        value = fold(product, rhs, rank) + down[parent * rhs : (parent + 1) * rhs]
        parent_local.append(value.astype(BF16).astype(F32))
    for parent in range(parents):
        down = spread_down(parent_local[parent], leaf_maps[parent], maps, mask, links, rhs)
        rows = slice(parent * links * rhs, (parent + 1) * links * rhs)
        local[rows, :] = (far[rows, :] + down).astype(BF16)

    def finish(step, carry):
        for inner in range(group):
            leaf = step * group + inner
            value = local[pl.ds(pl.multiple_of(leaf * rhs, rhs), rhs), :]
            partial[leaf] = partial[leaf] + dot(value, basis[leaf])
        return carry

    lax.fori_loop(0, leaves // group, finish, 0)
    own[7].wait()
    settle((0, 1))


def near_kernel(
    grid_shape,
    near_list,
    near_count,
    points,
    charges,
    partial,
    potential,
    target_table,
    source_table,
    pair_source,
    pair_target,
):
    along = grid_shape[1]
    me = lax.axis_index("gx") * along + lax.axis_index("gy")
    _, leaves, rhs, size = charges.shape
    wide = 3 * leaves
    slots = near_list.shape[0] // leaves
    shift = leaves - me * leaves
    group = GROUP

    def list_leaf(leaf, count):
        used = near_count[leaf]
        rank_of = 0
        for slot in range(slots):
            source = near_list[leaf * slots + slot] + shift
            live = slot < used
            inside = (source >= leaves) & (source < 2 * leaves) & live
            done = inside & (rank_of < EARLY)
            pair_source[count] = source
            pair_target[count] = leaf
            count = count + jnp.where(live & jnp.logical_not(done), 1, 0)
            rank_of = rank_of + jnp.where(inside, 1, 0)
        return count

    pairs = lax.fori_loop(0, leaves, list_leaf, 0)
    for extra in range(group):
        pair_source[pairs + extra] = leaves
        pair_target[pairs + extra] = 0

    for block in range(3):
        for start in range(0, leaves, 16):
            coordinates = [points[block, axis, start : start + 16, :].astype(F32) for axis in range(3)]
            source_rows, target_rows = augmented(coordinates)
            put_rows(source_table, source_rows, block * leaves + start, wide)
            if block == 1:
                put_rows(target_table, target_rows, start, leaves)
    potential[...] = partial[...]

    def some_pairs(step, carry):
        results = []
        for inner in range(group):
            at = step * group + inner
            source = pair_source[at]
            target = pair_target[at]
            tile = near_tile(side_of(target_table, target, leaves), side_of(source_table, source, wide))
            value = dot(tile, charges[source // leaves, source % leaves], 1, 1).T
            results.append((target, jnp.where(at < pairs, value, 0.0)))
        for target, value in results:
            potential[target] = potential[target] + value
        return carry

    lax.fori_loop(0, (pairs + group - 1) // group, some_pairs, 0)


def stored(matrix, links):
    length = matrix.shape[-1]
    tiles = length // 128
    value = matrix.reshape(-1, links, tiles, 128).transpose(0, 2, 1, 3)
    return value.reshape(-1, tiles * links, 128)


def on_device(
    grid_shape,
    points,
    charges,
    near_list,
    near_count,
    far_leaf,
    far_cluster,
    basis,
    leaf_transfer,
    cluster_transfer,
    leaf_coupling,
    cluster_coupling,
    top_transfer,
    top_coupling,
):
    leaves, rhs, size = charges.shape
    rank = basis.shape[1]
    parents = cluster_transfer.shape[0]
    links = far_leaf.shape[1]
    levels = (grid_shape[0] * grid_shape[1]).bit_length() - 1
    turned = points.transpose(1, 0, 2)
    leaf_maps = stored(leaf_transfer, links)
    parent_maps = stored(cluster_transfer, links)[0]
    leaf_couplings = stored(leaf_coupling, links)
    parent_couplings = stored(cluster_coupling, links)
    vmem = pl.BlockSpec(memory_space=pltpu.VMEM)
    smem = pl.BlockSpec(memory_space=pltpu.SMEM)
    hbm = pl.BlockSpec(memory_space=pl.ANY)
    shape = jax.ShapeDtypeStruct
    near_flat = near_list.reshape(-1)
    slots = near_list.shape[1]
    spread = rank // 2 * links
    halves = size // 128
    wide_points, wide_charges, partial = pl.pallas_call(
        functools.partial(exchange_kernel, grid_shape),
        out_shape=(
            shape((3,) + turned.shape, BF16),
            shape((3,) + charges.shape, BF16),
            shape((leaves, rhs, size), F32),
        ),
        in_specs=[smem] * 4 + [vmem] * 2 + [hbm] * 7,
        out_specs=(vmem, vmem, vmem),
        scratch_shapes=[
            pltpu.VMEM((3, leaves * rhs, rank), BF16),
            pltpu.VMEM((3, parents * rhs, rank), BF16),
            pltpu.VMEM(charges.shape, BF16),
            pltpu.VMEM(basis.shape, BF16),
            pltpu.VMEM(leaf_maps.shape, BF16),
            pltpu.VMEM(parent_maps.shape, BF16),
            pltpu.VMEM(parent_couplings.shape, BF16),
            pltpu.VMEM(leaf_couplings.shape, BF16),
            pltpu.VMEM((halves * ROWS * leaves, 128), F32),
            pltpu.VMEM((halves * ROWS * leaves, 128), F32),
            pltpu.VMEM((leaves, ROWS, size), BF16),
            pltpu.VMEM((leaves, ROWS, size), BF16),
            pltpu.VMEM((3 * leaves, 2 * rhs, spread), BF16),
            pltpu.VMEM((3 * parents, 2 * rhs, spread), BF16),
            pltpu.VMEM((leaves * rhs, rank), F32),
            pltpu.VMEM((leaves * rhs, rank), BF16),
            pltpu.VMEM((levels, rhs, rank), BF16),
            pltpu.VMEM((levels, rhs, rank), BF16),
            pltpu.SemaphoreType.DMA((4, 2)),
            pltpu.SemaphoreType.DMA((4, 2)),
            pltpu.SemaphoreType.DMA((levels,)),
            pltpu.SemaphoreType.DMA((levels,)),
            pltpu.SemaphoreType.DMA((8,)),
        ],
        compiler_params=pltpu.CompilerParams(
            collective_id=0, has_side_effects=True, vmem_limit_bytes=48 << 20
        ),
        name="exchange",
    )(
        near_flat,
        near_count,
        far_leaf.reshape(-1),
        far_cluster.reshape(-1),
        top_transfer,
        top_coupling,
        turned,
        charges,
        basis,
        leaf_maps,
        parent_maps,
        parent_couplings,
        leaf_couplings,
    )
    return pl.pallas_call(
        functools.partial(near_kernel, grid_shape),
        out_shape=shape((leaves, rhs, size), F32),
        in_specs=[smem] * 2 + [vmem] * 3,
        out_specs=vmem,
        scratch_shapes=[
            pltpu.VMEM((halves * ROWS * leaves, 128), F32),
            pltpu.VMEM((halves * ROWS * 3 * leaves, 128), F32),
            pltpu.SMEM((leaves * slots + GROUP,), jnp.int32),
            pltpu.SMEM((leaves * slots + GROUP,), jnp.int32),
        ],
        compiler_params=pltpu.CompilerParams(vmem_limit_bytes=40 << 20),
        name="near",
    )(near_flat, near_count, wide_points, wide_charges, partial)


def solution(mesh):
    grid_shape = (mesh.shape["gx"], mesh.shape["gy"])
    both = ("gx", "gy")
    in_specs = (
        P(both, None, None),
        P(both, None, None),
        P(both, None),
        P(both),
        P(both, None),
        P(both, None),
        P(both, None, None),
        P(both, None),
        P(both, None),
        P(both, None, None),
        P(both, None, None),
        P(),
        P(),
    )
    return jax.shard_map(
        functools.partial(on_device, grid_shape),
        mesh=mesh,
        in_specs=in_specs,
        out_specs=P(both, None, None),
        check_vma=False,
    )
```
